256 devices in a mesh: wide: 16 (over y, x), narrow: 16 (over z, core).
Axes of the slice: x: 4, y: 4, z: 8, core: 2. Of those that a mesh axis runs over, the one named last changes fastest.
Arguments:
- anomalies: bfloat16 [256, 262144], P(None, ('wide', 'narrow')), may hold values from -16 to 16
- sketch: bfloat16 [128, 256], replicated, may hold values from -0.375 to 0.375
Outputs:
- eofs: float32 [128, 262144], P(None, ('wide', 'narrow'))
- pcs: float32 [128, 256], replicated
The draws below stay inside these ranges and needn't reach their ends.
All inputs are finite; a program needn't handle non-finite values.
Results may differ from the reference program's by a relative error of at most 0.0044.
Values may be sent and summed in bfloat16 or wider, within the bound.
No kernel may reach another device: no remote copies, remote signals or barrier semaphores. Data moves between devices by JAX's collectives and lax.ppermute only.
A program may use at most 64 MiB of HBM per device.

```python
import jax
import jax.numpy as jnp
from jax import lax

CELLS_PER_DEVICE = 1024
RECORD_DAYS = 256
RANK = 128
CELLS = 262144


def uniform_sample(key, shape):
    return jax.random.normal(key, shape, jnp.float32)


def draw_anomalies(key, part):
    block_list = CELLS // CELLS_PER_DEVICE
    block_days = RECORD_DAYS // block_list
    factors = min(RECORD_DAYS, CELLS // 8)
    ranks = jnp.arange(factors).astype(jnp.float32)
    spectrum = jnp.exp(-ranks * (jnp.log(jnp.float32(16.0)) / RANK))
    signal_strength = jnp.sqrt(jnp.float32(RECORD_DAYS) / jnp.sum(spectrum * spectrum))
    temporal = jnp.linalg.qr(jax.random.normal(jax.random.fold_in(key, 11), (RECORD_DAYS, factors), jnp.float32))[0]
    loading = temporal * (signal_strength * spectrum)[None, :]
    spread = jnp.log(jnp.float32(10.0))
    target_area = jnp.exp(jax.random.uniform(jax.random.fold_in(key, 12), (block_list,), jnp.float32) * spread)
    target_area = target_area / jnp.sqrt(jnp.mean(target_area * target_area))
    pairing = jax.random.permutation(jax.random.fold_in(key, 13), block_list).astype(jnp.int32)
    spike_length = 0.6 * signal_strength / 16.0 * jnp.sqrt(jnp.float32(block_list))
    day_block = (jnp.arange(RECORD_DAYS) // block_days).astype(jnp.int32)

    def one_block(position_index):
        block_random_key = jax.random.fold_in(key, position_index + 100)
        latent = uniform_sample(jax.random.fold_in(block_random_key, 1), (factors, CELLS_PER_DEVICE))
        background_noise = uniform_sample(jax.random.fold_in(block_random_key, 2), (RECORD_DAYS, CELLS_PER_DEVICE))
        event_spike = uniform_sample(jax.random.fold_in(block_random_key, 3), (RECORD_DAYS, CELLS_PER_DEVICE))
        spike_day_index = (day_block == pairing[position_index]).astype(jnp.float32)[:, None]
        signal_pattern = jnp.dot(loading, latent, precision=lax.Precision.HIGHEST)
        field_values = target_area[position_index] * (signal_pattern + 0.05 * background_noise + spike_length * spike_day_index * event_spike)
        return jnp.clip(field_values, -16.0, 16.0).astype(jnp.bfloat16)
    stacked = lax.map(one_block, jnp.arange(block_list).astype(jnp.int32))
    return jnp.transpose(stacked, (1, 0, 2)).reshape(RECORD_DAYS, CELLS)


def normal_values(own_key, dims, deviation, most, held_as=jnp.bfloat16):
    values = jax.random.normal(own_key, dims, jnp.float32) * deviation
    return jnp.minimum(jnp.maximum(values, -most), most).astype(held_as)


def setup_inputs(seed: int = 0) -> dict:
    splits = jax.random.split(jax.random.key(seed), 3)
    return {
        "anomalies": draw_anomalies(jax.random.fold_in(splits[2], 71), 0),
        "sketch": normal_values(splits[1], (RANK, RECORD_DAYS), RECORD_DAYS ** -0.5, 0.375),
    }


def outer_gram(matrix):
    return jnp.dot(matrix.astype(jnp.float32), matrix.T.astype(jnp.float32), precision=lax.Precision.HIGHEST, preferred_element_type=jnp.float32)

def lower_solve(lower_factor, matrix):
    return lax.linalg.triangular_solve(lower_factor, matrix, left_side=True, lower=True)

def orthonormal(matrix):
    lower_factor = jnp.linalg.cholesky(outer_gram(matrix))
    middle = lower_solve(lower_factor, matrix)
    second_lower = jnp.linalg.cholesky(outer_gram(middle))
    return lower_solve(second_lower, middle)

def project_days(rows, anomalies):
    return lax.dot_general(rows.astype(jnp.float32), anomalies.astype(jnp.float32), (((1,), (1,)), ((), ())), preferred_element_type=jnp.float32)

def reference(anomalies, sketch):
    first = jnp.dot(sketch.astype(jnp.float32), anomalies.astype(jnp.float32), preferred_element_type=jnp.float32)
    basis = orthonormal(first).astype(jnp.bfloat16)
    back = project_days(basis, anomalies).astype(jnp.bfloat16)
    second = jnp.dot(back.astype(jnp.float32), anomalies.astype(jnp.float32), preferred_element_type=jnp.float32)
    refined = orthonormal(second)
    day_scale = jnp.sqrt(jnp.float32(RECORD_DAYS) / jnp.float32(CELLS))
    pcs = project_days(refined.astype(jnp.bfloat16), anomalies) * day_scale
    eofs = refined * jnp.sqrt(jnp.float32(CELLS))
    return (eofs, pcs)
```

```python
import functools

import jax
import jax.numpy as jnp
from jax import lax
from jax.experimental import pallas as pl
from jax.experimental.pallas import tpu as pltpu
from jax.sharding import Mesh
from jax.sharding import PartitionSpec as P

PLANE = ("y", "x")
CELL_AXES = ("y", "x", "z", "core")
RANK = 128
DAYS = 256
SUB = 8
PANEL = 4
NEAR = 1e-4
HIGHEST = lax.Precision.HIGHEST


def dot(a, b, dims=((1,), (0,))):
    return lax.dot_general(
        a, b, (dims, ((), ())), precision=HIGHEST, preferred_element_type=jnp.float32
    )


def dot_nt(a, b):
    return dot(a, b, ((1,), (1,)))


def pieces(a):
    high = a.astype(jnp.bfloat16)
    rest = a - high.astype(jnp.float32)
    middle = rest.astype(jnp.bfloat16)
    low = (rest - middle.astype(jnp.float32)).astype(jnp.bfloat16)
    return high, middle, low


def dot_right(a, split, dims=((1,), (0,))):
    high, middle, low = (
        lax.dot_general(a, b, (dims, ((), ())), preferred_element_type=jnp.float32) for b in split
    )
    return high + (middle + low)


def dot_left(split, b, dims=((1,), (0,))):
    high, middle, low = (
        lax.dot_general(a, b, (dims, ((), ())), preferred_element_type=jnp.float32) for a in split
    )
    return high + (middle + low)


def spread(a):
    return jnp.broadcast_to(a, (SUB, RANK))


def eliminated(gram):
    lane = lax.broadcasted_iota(jnp.int32, (SUB, RANK), 1)
    sub = lax.broadcasted_iota(jnp.int32, (SUB, RANK), 0)
    rows = [gram[SUB * b : SUB * (b + 1), :] for b in range(RANK // SUB)]
    scales = []
    for b in range(RANK // SUB):
        scale = jnp.ones((SUB, RANK), jnp.float32)
        for k in range(0, SUB, PANEL):
            j = SUB * b + k
            top = [spread(rows[b][k + t : k + t + 1, :]) for t in range(PANEL)]
            s = {
                (t, u): spread(top[t][:, j + u : j + u + 1])
                for t in range(PANEL)
                for u in range(t, PANEL)
            }
            factor, ratio = [], {}
            for t in range(PANEL):
                inverse = 1.0 / s[t, t]
                scale = jnp.where(sub == k + t, s[t, t], scale)
                factor.append(jnp.where(lane == j + t, 1.0, top[t]) * inverse)
                for u in range(t + 1, PANEL):
                    ratio[t, u] = s[t, u] * inverse
                for u in range(t + 1, PANEL):
                    top[u] = jnp.where(lane == j + t, 0.0, top[u]) - s[t, u] * factor[t]
                    for v in range(u, PANEL):
                        s[u, v] = s[u, v] - ratio[t, u] * s[t, v]
            in_panel = (lane >= j) & (lane < j + PANEL)
            update = [
                jnp.where((lane > j + t) & (lane < j + PANEL), 0.0, factor[t])
                for t in range(PANEL)
            ]
            for i in range(b if k + PANEL < SUB else b + 1, RANK // SUB):
                column = [spread(rows[i][:, j + t : j + t + 1]) for t in range(PANEL)]
                for t in range(PANEL):
                    for u in range(t + 1, PANEL):
                        column[u] = column[u] - column[t] * ratio[t, u]
                total = column[0] * update[0]
                for t in range(1, PANEL):
                    total = total + column[t] * update[t]
                changed = jnp.where(in_panel, 0.0, rows[i]) - total
                if i == b:
                    changed = jnp.where(sub >= k + PANEL, changed, rows[i])
                rows[i] = changed
            for t in range(PANEL):
                rows[b] = jnp.where(sub == k + t, top[t], rows[b])
        scales.append(scale)
    out = []
    for b in range(RANK // SUB):
        place = lane - (sub + SUB * b)
        unit = jnp.where(place < 0, rows[b], jnp.where(place == 0, 1.0, 0.0))
        out.append(unit * lax.rsqrt(scales[b]))
    return jnp.concatenate(out, axis=0)


def half_lower(a, row, column):
    return jnp.where(row > column, a, jnp.where(row == column, 0.5 * a, 0.0))


def whitened(gram, out_ref):
    row = lax.broadcasted_iota(jnp.int32, (RANK, RANK), 0)
    column = lax.broadcasted_iota(jnp.int32, (RANK, RANK), 1)
    identity = jnp.where(row == column, 1.0, 0.0)
    error = gram - identity
    near = jnp.sum(error * error) < NEAR

    @pl.when(near)
    def _():
        first = identity - half_lower(error, row, column)
        left = dot_nt(dot(first, gram), first) - identity
        out_ref[...] = first - dot(half_lower(left, row, column), first)

    @pl.when(jnp.logical_not(near))
    def _():
        out_ref[...] = eliminated(gram)


def algebra(cells, mine_ref, other_ref, core_ref, sketch_ref, anomalies_ref, eofs_ref, pcs_ref, inv_ref):
    first_core = core_ref[0, 0] == 0
    mine, other = mine_ref[...], other_ref[...]
    covariance = jnp.concatenate(
        [jnp.where(first_core, mine, other), jnp.where(first_core, other, mine)], axis=1
    )
    parts = pieces(covariance)
    sketch = sketch_ref[...]
    seen = dot_right(sketch, parts)
    gram = dot_left(pieces(seen), sketch, ((1,), (1,)))
    inverse = eliminated(gram)
    rows = dot_left(pieces(inverse), sketch)
    whitened(dot_nt(dot(rows, covariance), rows), inv_ref)
    back = dot(inv_ref[...], dot(inverse, seen)).astype(jnp.bfloat16)
    gram = dot_left(pieces(dot_right(back, parts)), back, ((1,), (1,)))
    inverse = eliminated(gram)
    rows = dot_left(pieces(inverse), back)
    days = dot(rows, covariance)
    whitened(dot_nt(days, rows), inv_ref)
    inverse = inv_ref[...]
    pcs_ref[...] = dot(inverse, days) * jnp.sqrt(jnp.float32(DAYS) / jnp.float32(cells))
    refined = dot(inverse, rows)
    eofs_ref[...] = dot_left(pieces(refined), anomalies_ref[...]) * jnp.sqrt(jnp.float32(cells))


def exchanged(array):
    return lax.ppermute(array, "core", [(0, 1), (1, 0)])


def all_to_all(array, axes):
    return lax.all_to_all(array, axes, split_axis=0, concat_axis=0, tiled=True)


def sent_to_all(array, axes):
    return all_to_all(jnp.broadcast_to(array, (lax.axis_size(axes), *array.shape)), axes)


def summed_halves(anomalies):
    core = lax.axis_index("core")
    product = lax.dot_general(
        anomalies, anomalies, (((1,), (1,)), ((), ())), preferred_element_type=jnp.float32
    )
    halves = jnp.stack([product[:, :RANK], product[:, RANK:]])
    own = lax.dynamic_index_in_dim(halves, core, 0, False)
    partner = lax.dynamic_index_in_dim(halves, 1 - core, 0, False)
    half = own + exchanged(partner)
    count = lax.axis_size(PLANE)
    share = all_to_all(half.reshape(count, -1, RANK), PLANE).sum(axis=0)
    share = sent_to_all(share, "z").sum(axis=0)
    return sent_to_all(share, PLANE).reshape(DAYS, RANK)


def local(anomalies, sketch):
    mine = summed_halves(anomalies)
    other = exchanged(mine)
    core = lax.axis_index("core").astype(jnp.int32).reshape(1, 1)
    cells = anomalies.shape[1] * lax.axis_size(CELL_AXES)
    vmem = pl.BlockSpec(memory_space=pltpu.VMEM)
    smem = pl.BlockSpec(memory_space=pltpu.SMEM)
    return pl.pallas_call(
        functools.partial(algebra, cells),
        out_shape=(
            jax.ShapeDtypeStruct((RANK, anomalies.shape[1]), jnp.float32),
            jax.ShapeDtypeStruct((RANK, DAYS), jnp.float32),
        ),
        in_specs=[vmem, vmem, smem, vmem, vmem],
        out_specs=(vmem, vmem),
        scratch_shapes=[pltpu.VMEM((RANK, RANK), jnp.float32)],
        name="algebra",
    )(mine, other, core, sketch, anomalies)


def solution(mesh):
    split = Mesh(mesh.devices.reshape(4, 4, 8, 2), CELL_AXES)
    in_specs = (P(None, CELL_AXES), P())
    out_specs = (P(None, CELL_AXES), P())
    return jax.shard_map(local, mesh=split, in_specs=in_specs, out_specs=out_specs, check_vma=False)
```

```python
import functools

import jax
import jax.numpy as jnp
from jax import lax
from jax.experimental import pallas as pl
from jax.experimental.pallas import tpu as pltpu
from jax.sharding import Mesh
from jax.sharding import PartitionSpec as P

PLANE = ("y", "x")
CELL_AXES = ("y", "x", "z", "core")
RANK = 128
DAYS = 256
SUB = 8
PANEL = 16
NEAR = 1e-5
HIGHEST = lax.Precision.HIGHEST


def dot(a, b, dims=((1,), (0,))):
    return lax.dot_general(
        a, b, (dims, ((), ())), precision=HIGHEST, preferred_element_type=jnp.float32
    )


def dot_nt(a, b):
    return dot(a, b, ((1,), (1,)))


def pieces(a):
    high = a.astype(jnp.bfloat16)
    rest = a - high.astype(jnp.float32)
    middle = rest.astype(jnp.bfloat16)
    low = (rest - middle.astype(jnp.float32)).astype(jnp.bfloat16)
    return high, middle, low


def dot_right(a, split, dims=((1,), (0,))):
    high, middle, low = (
        lax.dot_general(a, b, (dims, ((), ())), preferred_element_type=jnp.float32) for b in split
    )
    return high + (middle + low)


def dot_left(split, b, dims=((1,), (0,))):
    high, middle, low = (
        lax.dot_general(a, b, (dims, ((), ())), preferred_element_type=jnp.float32) for a in split
    )
    return high + (middle + low)


def spread(a):
    return jnp.broadcast_to(a, (SUB, RANK))


def eliminated(gram):
    lane = lax.broadcasted_iota(jnp.int32, (SUB, RANK), 1)
    sub = lax.broadcasted_iota(jnp.int32, (SUB, RANK), 0)
    at = [sub == s for s in range(SUB)]
    count, tall = RANK // SUB, PANEL // SUB
    rows = [gram[SUB * b : SUB * (b + 1), :] for b in range(count)]
    scales = []
    for p in range(0, count, tall):
        j = SUB * p
        block = rows[p : p + tall]
        kept, scale = list(block), [jnp.ones((SUB, RANK), jnp.float32)] * tall
        columns = [[spread(a[:, j + u : j + u + 1]) for a in block] for u in range(PANEL)]
        pivot = spread(columns[0][0][0:1, :])
        for t in range(PANEL):
            own, s = divmod(t, SUB)
            inverse = 1.0 / pivot
            scale[own] = jnp.where(at[s], pivot, scale[own])
            across = {v: spread(columns[v][own][s : s + 1, :]) for v in range(t + 1, PANEL)}
            if t + 1 < PANEL:
                b, r = divmod(t + 1, SUB)
                corner = spread(columns[t + 1][b][r : r + 1, :])
                pivot = corner - (across[t + 1] * across[t + 1]) * inverse
            row = spread(block[own][s : s + 1, :])
            kept[own] = jnp.where(at[s], row, kept[own])
            here = lane == j + t
            row = jnp.where(here, 1.0, row)
            for k in range(tall):
                changed = jnp.where(here, 0.0, block[k]) - (columns[t][k] * row) * inverse
                block[k] = jnp.where(at[s], row * inverse, changed) if k == own else changed
            for v in range(t + 1, PANEL):
                for k in range(tall):
                    changed = columns[v][k] - (columns[t][k] * across[v]) * inverse
                    if k == own:
                        changed = jnp.where(at[s], across[v] * inverse, changed)
                    columns[v][k] = changed
        rows[p : p + tall] = kept
        scales += scale
        solved = [spread(block[u // SUB][u % SUB : u % SUB + 1, :]) for u in range(PANEL)]
        inside = (lane >= j) & (lane < j + PANEL)
        for i in range(p + tall, count):
            terms = [spread(rows[i][:, j + u : j + u + 1]) * solved[u] for u in range(PANEL)]
            while len(terms) > 1:
                terms = [terms[k] + terms[k + 1] for k in range(0, len(terms), 2)]
            rows[i] = jnp.where(inside, 0.0, rows[i]) - terms[0]
    out = []
    for b in range(count):
        place = lane - (sub + SUB * b)
        unit = jnp.where(place < 0, rows[b], jnp.where(place == 0, 1.0, 0.0))
        out.append(unit * lax.rsqrt(scales[b]))
    return jnp.concatenate(out, axis=0)


def half_lower(a, row, column):
    return jnp.where(row > column, a, jnp.where(row == column, 0.5 * a, 0.0))


def correction(gram, out_ref):
    row = lax.broadcasted_iota(jnp.int32, (RANK, RANK), 0)
    column = lax.broadcasted_iota(jnp.int32, (RANK, RANK), 1)
    identity = jnp.where(row == column, 1.0, 0.0)
    error = gram - identity
    near = jnp.sum(error * error) < NEAR

    @pl.when(near)
    def _():
        first = half_lower(error, row, column)
        small = first.astype(jnp.bfloat16)
        square = jnp.dot(small, small, preferred_element_type=jnp.float32)
        outer = lax.dot_general(
            small, small, (((1,), (1,)), ((), ())), preferred_element_type=jnp.float32
        )
        out_ref[...] = (square + half_lower(outer, row, column)) - first

    @pl.when(jnp.logical_not(near))
    def _():
        out_ref[...] = eliminated(gram) - identity


def two(a):
    high = a.astype(jnp.bfloat16)
    return high, (a - high.astype(jnp.float32)).astype(jnp.bfloat16)


def corrected(change, array):
    change_high, change_low = change
    high, low = two(array)
    product = functools.partial(jnp.dot, preferred_element_type=jnp.float32)
    return array + (
        product(change_high, high) + (product(change_high, low) + product(change_low, high))
    )


def algebra(cells, mine_ref, other_ref, core_ref, sketch_ref, anomalies_ref, eofs_ref, pcs_ref, change_ref):
    first_core = core_ref[0, 0] == 0
    mine, other = mine_ref[...], other_ref[...]
    covariance = jnp.concatenate(
        [jnp.where(first_core, mine, other), jnp.where(first_core, other, mine)], axis=1
    )
    parts = pieces(covariance)
    sketch = sketch_ref[...]
    seen = dot_right(sketch, parts)
    gram = dot_left(pieces(seen), sketch, ((1,), (1,)))
    inverse = eliminated(gram)
    days = dot(inverse, seen)
    correction(dot_nt(days, dot_left(pieces(inverse), sketch)), change_ref)
    back = corrected(two(change_ref[...]), days).astype(jnp.bfloat16)
    gram = dot_left(pieces(dot_right(back, parts)), back, ((1,), (1,)))
    inverse = eliminated(gram)
    rows = dot_left(pieces(inverse), back)
    days = dot(rows, covariance)
    patterns = dot_left(pieces(rows), anomalies_ref[...])
    correction(dot_nt(days, rows), change_ref)
    change = two(change_ref[...])
    pcs_ref[...] = corrected(change, days) * jnp.sqrt(jnp.float32(DAYS) / jnp.float32(cells))
    eofs_ref[...] = corrected(change, patterns) * jnp.sqrt(jnp.float32(cells))


def exchanged(array):
    return lax.ppermute(array, "core", [(0, 1), (1, 0)])


def all_to_all(array, axes):
    return lax.all_to_all(array, axes, split_axis=0, concat_axis=0, tiled=True)


def sent_to_all(array, axes):
    return all_to_all(jnp.broadcast_to(array, (lax.axis_size(axes), *array.shape)), axes)


def summed_halves(anomalies):
    core = lax.axis_index("core")
    product = lax.dot_general(
        anomalies, anomalies, (((1,), (1,)), ((), ())), preferred_element_type=jnp.float32
    )
    halves = jnp.stack([product[:, :RANK], product[:, RANK:]])
    own = lax.dynamic_index_in_dim(halves, core, 0, False)
    partner = lax.dynamic_index_in_dim(halves, 1 - core, 0, False)
    half = own + exchanged(partner)
    count = lax.axis_size(PLANE)
    share = all_to_all(half.reshape(count, -1, RANK), PLANE).sum(axis=0)
    share = sent_to_all(share, "z").sum(axis=0)
    return sent_to_all(share, PLANE).reshape(DAYS, RANK)


def local(anomalies, sketch):
    mine = summed_halves(anomalies)
    other = exchanged(mine)
    core = lax.axis_index("core").astype(jnp.int32).reshape(1, 1)
    cells = anomalies.shape[1] * lax.axis_size(CELL_AXES)
    vmem = pl.BlockSpec(memory_space=pltpu.VMEM)
    smem = pl.BlockSpec(memory_space=pltpu.SMEM)
    return pl.pallas_call(
        functools.partial(algebra, cells),
        out_shape=(
            jax.ShapeDtypeStruct((RANK, anomalies.shape[1]), jnp.float32),
            jax.ShapeDtypeStruct((RANK, DAYS), jnp.float32),
        ),
        in_specs=[vmem, vmem, smem, vmem, vmem],
        out_specs=(vmem, vmem),
        scratch_shapes=[pltpu.VMEM((RANK, RANK), jnp.float32)],
        compiler_params=pltpu.CompilerParams(vmem_limit_bytes=16 * 2**20),
        name="algebra",
    )(mine, other, core, sketch, anomalies)


def solution(mesh):
    split = Mesh(mesh.devices.reshape(4, 4, 8, 2), CELL_AXES)
    in_specs = (P(None, CELL_AXES), P())
    out_specs = (P(None, CELL_AXES), P())
    return jax.shard_map(local, mesh=split, in_specs=in_specs, out_specs=out_specs, check_vma=False)
```

```python
import functools

import jax
import jax.numpy as jnp
from jax import lax
from jax.experimental import pallas as pl
from jax.experimental.pallas import tpu as pltpu
from jax.sharding import Mesh
from jax.sharding import PartitionSpec as P

LAYER = ("y", "x", "core")
CELL_AXES = ("y", "x", "z", "core")
RANK = 128
DAYS = 256
PRODUCT_VMEM = 8 * 2**20
PACKED = 288
SUB = 8
PANEL = 16
NEAR = 2e-5
HIGHEST = lax.Precision.HIGHEST


def dot(a, b, dims=((1,), (0,))):
    return lax.dot_general(
        a, b, (dims, ((), ())), precision=HIGHEST, preferred_element_type=jnp.float32
    )


def dot_nt(a, b):
    return dot(a, b, ((1,), (1,)))


def pieces(a):
    high = a.astype(jnp.bfloat16)
    rest = a - high.astype(jnp.float32)
    middle = rest.astype(jnp.bfloat16)
    low = (rest - middle.astype(jnp.float32)).astype(jnp.bfloat16)
    return high, middle, low


def dot_right(a, split, dims=((1,), (0,))):
    high, middle, low = (
        lax.dot_general(a, b, (dims, ((), ())), preferred_element_type=jnp.float32) for b in split
    )
    return high + (middle + low)


def dot_left(split, b, dims=((1,), (0,))):
    high, middle, low = (
        lax.dot_general(a, b, (dims, ((), ())), preferred_element_type=jnp.float32) for a in split
    )
    return high + (middle + low)


def spread(a):
    return jnp.broadcast_to(a, (SUB, RANK))


def eliminated(gram):
    lane = lax.broadcasted_iota(jnp.int32, (SUB, RANK), 1)
    sub = lax.broadcasted_iota(jnp.int32, (SUB, RANK), 0)
    at = [sub == s for s in range(SUB)]
    count, tall = RANK // SUB, PANEL // SUB
    rows = [gram[SUB * b : SUB * (b + 1), :] for b in range(count)]
    scales = []
    for p in range(0, count, tall):
        j = SUB * p
        block = rows[p : p + tall]
        kept, scale = list(block), [jnp.ones((SUB, RANK), jnp.float32)] * tall
        columns = [[spread(a[:, j + u : j + u + 1]) for a in block] for u in range(PANEL)]
        pivot = spread(columns[0][0][0:1, :])
        for t in range(PANEL):
            own, s = divmod(t, SUB)
            inverse = 1.0 / pivot
            scale[own] = jnp.where(at[s], pivot, scale[own])
            across = {v: spread(columns[v][own][s : s + 1, :]) for v in range(t + 1, PANEL)}
            if t + 1 < PANEL:
                b, r = divmod(t + 1, SUB)
                corner = spread(columns[t + 1][b][r : r + 1, :])
                pivot = corner - (across[t + 1] * across[t + 1]) * inverse
            row = spread(block[own][s : s + 1, :])
            kept[own] = jnp.where(at[s], row, kept[own])
            here = lane == j + t
            row = jnp.where(here, 1.0, row)
            for k in range(tall):
                changed = jnp.where(here, 0.0, block[k]) - (columns[t][k] * row) * inverse
                block[k] = jnp.where(at[s], row * inverse, changed) if k == own else changed
            for v in range(t + 1, PANEL):
                for k in range(tall):
                    changed = columns[v][k] - (columns[t][k] * across[v]) * inverse
                    if k == own:
                        changed = jnp.where(at[s], across[v] * inverse, changed)
                    columns[v][k] = changed
        rows[p : p + tall] = kept
        scales += scale
        solved = [spread(block[u // SUB][u % SUB : u % SUB + 1, :]) for u in range(PANEL)]
        inside = (lane >= j) & (lane < j + PANEL)
        for i in range(p + tall, count):
            terms = [spread(rows[i][:, j + u : j + u + 1]) * solved[u] for u in range(PANEL)]
            while len(terms) > 1:
                terms = [terms[k] + terms[k + 1] for k in range(0, len(terms), 2)]
            rows[i] = jnp.where(inside, 0.0, rows[i]) - terms[0]
    out = []
    for b in range(count):
        place = lane - (sub + SUB * b)
        unit = jnp.where(place < 0, rows[b], jnp.where(place == 0, 1.0, 0.0))
        out.append(unit * lax.rsqrt(scales[b]))
    return jnp.concatenate(out, axis=0)


def eliminated_slowly(gram):
    row = lax.broadcasted_iota(jnp.int32, (RANK, RANK), 0)
    column = lax.broadcasted_iota(jnp.int32, (RANK, RANK), 1)

    def step(j, a):
        across = jnp.sum(jnp.where(row == j, a, 0.0), axis=0, keepdims=True)
        down = jnp.sum(jnp.where(column == j, a, 0.0), axis=1, keepdims=True)
        pivot = jnp.sum(jnp.where(column == row, jnp.where(row == j, a, 0.0), 0.0))
        across = jnp.where(column == j, 1.0, across) / pivot
        return jnp.where(row > j, jnp.where(column == j, 0.0, a) - down * across, a)

    a = lax.fori_loop(0, RANK, step, gram)
    pivots = jnp.sum(jnp.where(row == column, a, 0.0), axis=1, keepdims=True)
    unit = jnp.where(row > column, a, jnp.where(row == column, 1.0, 0.0))
    return unit * lax.rsqrt(pivots)


def identity():
    row = lax.broadcasted_iota(jnp.int32, (RANK, RANK), 0)
    column = lax.broadcasted_iota(jnp.int32, (RANK, RANK), 1)
    return jnp.where(row == column, 1.0, 0.0)


def half_lower(a):
    row = lax.broadcasted_iota(jnp.int32, (RANK, RANK), 0)
    column = lax.broadcasted_iota(jnp.int32, (RANK, RANK), 1)
    return jnp.where(row > column, a, jnp.where(row == column, 0.5 * a, 0.0))


def series(gram):
    error = gram - identity()
    first = half_lower(error)
    small = first.astype(jnp.bfloat16)
    square = jnp.dot(small, small, preferred_element_type=jnp.float32)
    outer = lax.dot_general(
        small, small, (((1,), (1,)), ((), ())), preferred_element_type=jnp.float32
    )
    return (square + half_lower(outer)) - first, jnp.sum(error * error)


def whole(gram):
    return eliminated_slowly(gram) - identity(), None


def two(a):
    high = a.astype(jnp.bfloat16)
    return high, (a - high.astype(jnp.float32)).astype(jnp.bfloat16)


def corrected(change, array):
    change_high, change_low = change
    high, low = two(array)
    product = functools.partial(jnp.dot, preferred_element_type=jnp.float32)
    return array + (
        product(change_high, high) + (product(change_high, low) + product(change_low, high))
    )


def unpacked(packed):
    row = lax.broadcasted_iota(jnp.int32, (RANK, RANK), 0)
    column = lax.broadcasted_iota(jnp.int32, (RANK, RANK), 1)
    corner, both = packed[:RANK, :], packed[RANK:DAYS, :]
    flipped = both.T
    diagonal = packed[DAYS : DAYS + 1, :]
    first = jnp.where(row >= column, both, flipped)
    last = jnp.where(row < column, both, jnp.where(row == column, diagonal, flipped))
    return jnp.concatenate(
        [jnp.concatenate([first, corner], axis=1), jnp.concatenate([corner.T, last], axis=1)],
        axis=0,
    )


def outputs(cells, first_factor, second_factor, refs):
    packed_ref, sketch_ref, anomalies_ref, eofs_ref, pcs_ref = refs
    covariance = unpacked(packed_ref[...])
    parts = pieces(covariance)
    sketch = sketch_ref[...]
    seen = dot_right(sketch, parts)
    gram = dot_left(pieces(seen), sketch, ((1,), (1,)))
    inverse = first_factor(gram)
    days = dot(inverse, seen)
    change, first_error = second_factor(dot_nt(days, dot_left(pieces(inverse), sketch)))
    back = corrected(two(change), days).astype(jnp.bfloat16)
    gram = dot_left(pieces(dot_right(back, parts)), back, ((1,), (1,)))
    inverse = first_factor(gram)
    rows = dot_left(pieces(inverse), back)
    days = dot(rows, covariance)
    patterns = dot_left(pieces(rows), anomalies_ref[...])
    change, last_error = second_factor(dot_nt(days, rows))
    change = two(change)
    pcs_ref[...] = corrected(change, days) * jnp.sqrt(jnp.float32(DAYS) / jnp.float32(cells))
    eofs_ref[...] = corrected(change, patterns) * jnp.sqrt(jnp.float32(cells))
    return first_error, last_error


def algebra(cells, *refs):
    first_error, last_error = outputs(cells, eliminated, series, refs)

    @pl.when(jnp.logical_not((first_error < NEAR) & (last_error < NEAR)))
    def _():
        outputs(cells, eliminated_slowly, whole, refs)


def product(anomalies_ref, packed_ref, here, arrived):
    copy = pltpu.make_async_copy(anomalies_ref, here, arrived)
    copy.start()
    copy.wait()
    cells = here[...]
    total = lax.dot_general(
        cells, cells, (((1,), (1,)), ((), ())), preferred_element_type=jnp.float32
    )
    row = lax.broadcasted_iota(jnp.int32, (RANK, RANK), 0)
    column = lax.broadcasted_iota(jnp.int32, (RANK, RANK), 1)
    first, last = total[:RANK, :RANK], total[RANK:, RANK:]
    diagonal = jnp.sum(jnp.where(row == column, last, 0.0), axis=0, keepdims=True)
    packed_ref[:RANK, :] = total[:RANK, RANK:]
    packed_ref[RANK:DAYS, :] = jnp.where(row >= column, first, last)
    spare = lax.broadcasted_iota(jnp.int32, (PACKED - DAYS, RANK), 0)
    packed_ref[DAYS:, :] = jnp.where(spare == 0, diagonal, 0.0)


def all_to_all(array, axes):
    return lax.all_to_all(array, axes, split_axis=0, concat_axis=0, tiled=True)


def sent_to_all(array, axes):
    return all_to_all(jnp.broadcast_to(array, (lax.axis_size(axes), *array.shape)), axes)


def summed(packed):
    shares = packed.reshape(lax.axis_size(LAYER), -1, 1, RANK)
    share = all_to_all(shares, LAYER).sum(axis=0)
    share = sent_to_all(share, "z").sum(axis=0)
    return sent_to_all(share, LAYER).reshape(packed.shape)


def local(anomalies, sketch):
    cells = anomalies.shape[1] * lax.axis_size(CELL_AXES)
    vmem = pl.BlockSpec(memory_space=pltpu.VMEM)
    packed = pl.pallas_call(
        product,
        out_shape=jax.ShapeDtypeStruct((PACKED, RANK), jnp.float32),
        in_specs=[pl.BlockSpec(memory_space=pltpu.HBM)],
        out_specs=vmem,
        scratch_shapes=[pltpu.VMEM(anomalies.shape, anomalies.dtype), pltpu.SemaphoreType.DMA],
        compiler_params=pltpu.CompilerParams(vmem_limit_bytes=PRODUCT_VMEM),
        name="product",
    )(pltpu.with_memory_space_constraint(anomalies, pltpu.HBM))
    return pl.pallas_call(
        functools.partial(algebra, cells),
        out_shape=(
            jax.ShapeDtypeStruct((RANK, anomalies.shape[1]), jnp.float32),
            jax.ShapeDtypeStruct((RANK, DAYS), jnp.float32),
        ),
        in_specs=[vmem, vmem, vmem],
        out_specs=(vmem, vmem),
        compiler_params=pltpu.CompilerParams(vmem_limit_bytes=16 * 2**20),
        name="algebra",
    )(summed(packed), sketch, anomalies)


def solution(mesh):
    split = Mesh(mesh.devices.reshape(4, 4, 8, 2), CELL_AXES)
    in_specs = (P(None, CELL_AXES), P())
    out_specs = (P(None, CELL_AXES), P())
    return jax.shard_map(local, mesh=split, in_specs=in_specs, out_specs=out_specs, check_vma=False)
```

```python
import functools

import jax
import jax.numpy as jnp
from jax import lax
from jax.experimental import pallas as pl
from jax.experimental.pallas import tpu as pltpu
from jax.sharding import Mesh
from jax.sharding import PartitionSpec as P

LAYER = ("y", "x", "core")
CELL_AXES = ("y", "x", "z", "core")
RANK = 128
DAYS = 256
PRODUCT_VMEM = 8 * 2**20
PACKED = 288
SUB = 8
PANEL = 16
NEAR = {1: 1e-7, 2: 2e-5}
HIGHEST = lax.Precision.HIGHEST


def dot(a, b, dims=((1,), (0,))):
    return lax.dot_general(
        a, b, (dims, ((), ())), precision=HIGHEST, preferred_element_type=jnp.float32
    )


def dot_nt(a, b):
    return dot(a, b, ((1,), (1,)))


def pieces(a):
    high = a.astype(jnp.bfloat16)
    rest = a - high.astype(jnp.float32)
    middle = rest.astype(jnp.bfloat16)
    low = (rest - middle.astype(jnp.float32)).astype(jnp.bfloat16)
    return high, middle, low


def dot_right(a, split, dims=((1,), (0,))):
    high, middle, low = (
        lax.dot_general(a, b, (dims, ((), ())), preferred_element_type=jnp.float32) for b in split
    )
    return high + (middle + low)


def dot_left(split, b, dims=((1,), (0,))):
    high, middle, low = (
        lax.dot_general(a, b, (dims, ((), ())), preferred_element_type=jnp.float32) for a in split
    )
    return high + (middle + low)


def spread(a):
    return jnp.broadcast_to(a, (SUB, RANK))


def eliminated(gram):
    lane = lax.broadcasted_iota(jnp.int32, (SUB, RANK), 1)
    sub = lax.broadcasted_iota(jnp.int32, (SUB, RANK), 0)
    at = [sub == s for s in range(SUB)]
    count, tall = RANK // SUB, PANEL // SUB
    rows = [gram[SUB * b : SUB * (b + 1), :] for b in range(count)]
    scales = []
    for p in range(0, count, tall):
        j = SUB * p
        block = rows[p : p + tall]
        kept, scale = list(block), [jnp.ones((SUB, RANK), jnp.float32)] * tall
        columns = [[spread(a[:, j + u : j + u + 1]) for a in block] for u in range(PANEL)]
        pivot = spread(columns[0][0][0:1, :])
        for t in range(PANEL):
            own, s = divmod(t, SUB)
            inverse = 1.0 / pivot
            scale[own] = jnp.where(at[s], pivot, scale[own])
            across = {v: spread(columns[v][own][s : s + 1, :]) for v in range(t + 1, PANEL)}
            if t + 1 < PANEL:
                b, r = divmod(t + 1, SUB)
                corner = spread(columns[t + 1][b][r : r + 1, :])
                pivot = corner - (across[t + 1] * across[t + 1]) * inverse
            row = spread(block[own][s : s + 1, :])
            kept[own] = jnp.where(at[s], row, kept[own])
            here = lane == j + t
            row = jnp.where(here, 1.0, row) * inverse
            for k in range(tall):
                changed = jnp.where(here, 0.0, block[k]) - columns[t][k] * row
                block[k] = jnp.where(at[s], row, changed) if k == own else changed
            for v in range(t + 1, PANEL):
                ratio = across[v] * inverse
                for k in range(tall):
                    changed = columns[v][k] - columns[t][k] * ratio
                    columns[v][k] = jnp.where(at[s], ratio, changed) if k == own else changed
        rows[p : p + tall] = kept
        scales += scale
        solved = [spread(block[u // SUB][u % SUB : u % SUB + 1, :]) for u in range(PANEL)]
        inside = (lane >= j) & (lane < j + PANEL)
        for i in range(p + tall, count):
            terms = [spread(rows[i][:, j + u : j + u + 1]) * solved[u] for u in range(PANEL)]
            while len(terms) > 1:
                terms = [terms[k] + terms[k + 1] for k in range(0, len(terms), 2)]
            rows[i] = jnp.where(inside, 0.0, rows[i]) - terms[0]
    out = []
    for b in range(count):
        place = lane - (sub + SUB * b)
        unit = jnp.where(place < 0, rows[b], jnp.where(place == 0, 1.0, 0.0))
        out.append(unit * lax.rsqrt(scales[b]))
    return jnp.concatenate(out, axis=0)


def eliminated_slowly(gram):
    row = lax.broadcasted_iota(jnp.int32, (RANK, RANK), 0)
    column = lax.broadcasted_iota(jnp.int32, (RANK, RANK), 1)

    def step(j, a):
        across = jnp.sum(jnp.where(row == j, a, 0.0), axis=0, keepdims=True)
        down = jnp.sum(jnp.where(column == j, a, 0.0), axis=1, keepdims=True)
        pivot = jnp.sum(jnp.where(column == row, jnp.where(row == j, a, 0.0), 0.0))
        across = jnp.where(column == j, 1.0, across) / pivot
        return jnp.where(row > j, jnp.where(column == j, 0.0, a) - down * across, a)

    a = lax.fori_loop(0, RANK, step, gram)
    pivots = jnp.sum(jnp.where(row == column, a, 0.0), axis=1, keepdims=True)
    unit = jnp.where(row > column, a, jnp.where(row == column, 1.0, 0.0))
    return unit * lax.rsqrt(pivots)


def identity():
    row = lax.broadcasted_iota(jnp.int32, (RANK, RANK), 0)
    column = lax.broadcasted_iota(jnp.int32, (RANK, RANK), 1)
    return jnp.where(row == column, 1.0, 0.0)


def half_lower(a):
    row = lax.broadcasted_iota(jnp.int32, (RANK, RANK), 0)
    column = lax.broadcasted_iota(jnp.int32, (RANK, RANK), 1)
    return jnp.where(row > column, a, jnp.where(row == column, 0.5 * a, 0.0))


def series(gram, order):
    error = gram - identity()
    near = jnp.sum(error * error) < NEAR[order]
    first = half_lower(error)
    if order == 1:
        return -first, near
    small = first.astype(jnp.bfloat16)
    square = jnp.dot(small, small, preferred_element_type=jnp.float32)
    outer = lax.dot_general(
        small, small, (((1,), (1,)), ((), ())), preferred_element_type=jnp.float32
    )
    return (square + half_lower(outer)) - first, near


def whole(gram, order):
    return eliminated_slowly(gram) - identity(), None


def two(a):
    high = a.astype(jnp.bfloat16)
    return high, (a - high.astype(jnp.float32)).astype(jnp.bfloat16)


def corrected(change, array):
    change_high, change_low = change
    high, low = two(array)
    product = functools.partial(jnp.dot, preferred_element_type=jnp.float32)
    return array + (
        product(change_high, high) + (product(change_high, low) + product(change_low, high))
    )


def unpacked(packed):
    row = lax.broadcasted_iota(jnp.int32, (RANK, RANK), 0)
    column = lax.broadcasted_iota(jnp.int32, (RANK, RANK), 1)
    corner, both = packed[:RANK, :], packed[RANK:DAYS, :]
    flipped = both.T
    diagonal = packed[DAYS : DAYS + 1, :]
    first = jnp.where(row >= column, both, flipped)
    last = jnp.where(row < column, both, jnp.where(row == column, diagonal, flipped))
    return jnp.concatenate(
        [jnp.concatenate([first, corner], axis=1), jnp.concatenate([corner.T, last], axis=1)],
        axis=0,
    )


def outputs(cells, first_factor, second_factor, refs):
    packed_ref, sketch_ref, anomalies_ref, eofs_ref, pcs_ref = refs
    covariance = unpacked(packed_ref[...])
    parts = pieces(covariance)
    sketch = sketch_ref[...]
    seen = dot_right(sketch, parts)
    gram = dot_left(pieces(seen), sketch, ((1,), (1,)))
    inverse = first_factor(gram)
    days = dot(inverse, seen)
    change, first_near = second_factor(dot_nt(days, dot_left(pieces(inverse), sketch)), 1)
    back = corrected(two(change), days).astype(jnp.bfloat16)
    seen = dot_right(back, parts)
    gram = dot_left(pieces(seen), back, ((1,), (1,)))
    inverse = first_factor(gram)
    rows = dot_left(pieces(inverse), back)
    days = dot(inverse, seen)
    patterns = dot_left(pieces(rows), anomalies_ref[...])
    change, last_near = second_factor(dot_nt(days, rows), 2)
    change = two(change)
    pcs_ref[...] = corrected(change, days) * jnp.sqrt(jnp.float32(DAYS) / jnp.float32(cells))
    eofs_ref[...] = corrected(change, patterns) * jnp.sqrt(jnp.float32(cells))
    return first_near, last_near


def algebra(cells, *refs):
    first_near, last_near = outputs(cells, eliminated, series, refs)

    @pl.when(jnp.logical_not(first_near & last_near))
    def _():
        outputs(cells, eliminated_slowly, whole, refs)


def product(anomalies_ref, packed_ref, here, arrived):
    copy = pltpu.make_async_copy(anomalies_ref, here, arrived)
    copy.start()
    copy.wait()
    cells = here[...]
    total = lax.dot_general(
        cells, cells, (((1,), (1,)), ((), ())), preferred_element_type=jnp.float32
    )
    row = lax.broadcasted_iota(jnp.int32, (RANK, RANK), 0)
    column = lax.broadcasted_iota(jnp.int32, (RANK, RANK), 1)
    first, last = total[:RANK, :RANK], total[RANK:, RANK:]
    diagonal = jnp.sum(jnp.where(row == column, last, 0.0), axis=0, keepdims=True)
    packed_ref[:RANK, :] = total[:RANK, RANK:]
    packed_ref[RANK:DAYS, :] = jnp.where(row >= column, first, last)
    spare = lax.broadcasted_iota(jnp.int32, (PACKED - DAYS, RANK), 0)
    packed_ref[DAYS:, :] = jnp.where(spare == 0, diagonal, 0.0)


def all_to_all(array, axes):
    return lax.all_to_all(array, axes, split_axis=0, concat_axis=0, tiled=True)


def sent_to_all(array, axes):
    return all_to_all(jnp.broadcast_to(array, (lax.axis_size(axes), *array.shape)), axes)


def summed(packed):
    shares = packed.reshape(lax.axis_size(LAYER), -1, 1, RANK)
    share = all_to_all(shares, LAYER).sum(axis=0)
    share = sent_to_all(share, "z").sum(axis=0)
    return sent_to_all(share, LAYER).reshape(packed.shape)


def local(anomalies, sketch):
    cells = anomalies.shape[1] * lax.axis_size(CELL_AXES)
    vmem = pl.BlockSpec(memory_space=pltpu.VMEM)
    packed = pl.pallas_call(
        product,
        out_shape=jax.ShapeDtypeStruct((PACKED, RANK), jnp.float32),
        in_specs=[pl.BlockSpec(memory_space=pltpu.HBM)],
        out_specs=vmem,
        scratch_shapes=[pltpu.VMEM(anomalies.shape, anomalies.dtype), pltpu.SemaphoreType.DMA],
        compiler_params=pltpu.CompilerParams(vmem_limit_bytes=PRODUCT_VMEM),
        name="product",
    )(pltpu.with_memory_space_constraint(anomalies, pltpu.HBM))
    return pl.pallas_call(
        functools.partial(algebra, cells),
        out_shape=(
            jax.ShapeDtypeStruct((RANK, anomalies.shape[1]), jnp.float32),
            jax.ShapeDtypeStruct((RANK, DAYS), jnp.float32),
        ),
        in_specs=[vmem, vmem, vmem],
        out_specs=(vmem, vmem),
        compiler_params=pltpu.CompilerParams(vmem_limit_bytes=16 * 2**20),
        name="algebra",
    )(summed(packed), sketch, anomalies)


def solution(mesh):
    split = Mesh(mesh.devices.reshape(4, 4, 8, 2), CELL_AXES)
    in_specs = (P(None, CELL_AXES), P())
    out_specs = (P(None, CELL_AXES), P())
    return jax.shard_map(local, mesh=split, in_specs=in_specs, out_specs=out_specs, check_vma=False)
```

```python
import functools

import jax
import jax.numpy as jnp
from jax import lax
from jax.experimental import pallas as pl
from jax.experimental.pallas import tpu as pltpu
from jax.sharding import Mesh
from jax.sharding import PartitionSpec as P

LAYER = ("y", "x", "core")
CELL_AXES = ("y", "x", "z", "core")
RANK = 128
DAYS = 256
PRODUCT_VMEM = 8 * 2**20
PACKED = 288
SUB = 8
PANEL = 16
NEAR = {1: 1e-7, 2: 2e-5}
HIGHEST = lax.Precision.HIGHEST


def dot(a, b, dims=((1,), (0,))):
    return lax.dot_general(
        a, b, (dims, ((), ())), precision=HIGHEST, preferred_element_type=jnp.float32
    )


def dot_nt(a, b):
    return dot(a, b, ((1,), (1,)))


def pieces(a):
    high = a.astype(jnp.bfloat16)
    rest = a - high.astype(jnp.float32)
    middle = rest.astype(jnp.bfloat16)
    low = (rest - middle.astype(jnp.float32)).astype(jnp.bfloat16)
    return high, middle, low


def dot_right(a, split, dims=((1,), (0,))):
    high, middle, low = (
        lax.dot_general(a, b, (dims, ((), ())), preferred_element_type=jnp.float32) for b in split
    )
    return high + (middle + low)


def dot_left(split, b, dims=((1,), (0,))):
    high, middle, low = (
        lax.dot_general(a, b, (dims, ((), ())), preferred_element_type=jnp.float32) for a in split
    )
    return high + (middle + low)


def spread(a):
    return jnp.broadcast_to(a, (SUB, RANK))


def eliminated(gram):
    lane = lax.broadcasted_iota(jnp.int32, (SUB, RANK), 1)
    sub = lax.broadcasted_iota(jnp.int32, (SUB, RANK), 0)
    at = [sub == s for s in range(SUB)]
    count, tall = RANK // SUB, PANEL // SUB
    rows = [gram[SUB * b : SUB * (b + 1), :] for b in range(count)]
    zeros = jnp.zeros((SUB, RANK), jnp.float32)
    scales = []
    for p in range(0, count, tall):
        j = SUB * p
        block = rows[p : p + tall]
        kept, scale = list(block), [jnp.ones((SUB, RANK), jnp.float32)] * tall
        columns = [[spread(a[:, j + u : j + u + 1]) for a in block] for u in range(PANEL)]
        pivot = spread(columns[0][0][0:1, :])
        for t in range(PANEL):
            own, s = divmod(t, SUB)
            inverse = 1.0 / pivot
            scale[own] = jnp.where(at[s], pivot, scale[own])
            across = {v: spread(columns[v][own][s : s + 1, :]) for v in range(t + 1, PANEL)}
            if t + 1 < PANEL:
                b, r = divmod(t + 1, SUB)
                corner = spread(columns[t + 1][b][r : r + 1, :])
                pivot = corner - (across[t + 1] * across[t + 1]) * inverse
            row = spread(block[own][s : s + 1, :])
            kept[own] = jnp.where(at[s], row, kept[own])
            here = lane == j + t
            row = jnp.where(here, 1.0, row) * inverse
            for k in range(tall):
                changed = jnp.where(here, 0.0, block[k]) - columns[t][k] * row
                block[k] = jnp.where(at[s], row, changed) if k == own else changed
            for v in range(t + 1, PANEL):
                ratio = across[v] * inverse
                for k in range(tall):
                    changed = columns[v][k] - columns[t][k] * ratio
                    columns[v][k] = jnp.where(at[s], ratio, changed) if k == own else changed
        rows[p : p + tall] = kept
        scales += scale
        inside = (lane >= j) & (lane < j + PANEL)
        behind = p + 2 * tall
        if p + tall < count:
            solved = [spread(block[u // SUB][u % SUB : u % SUB + 1, :]) for u in range(PANEL)]
            terms = {
                i: [spread(rows[i][:, j + u : j + u + 1]) * solved[u] for u in range(PANEL)]
                for i in range(p + tall, behind)
            }
            for i, total in terms.items():
                while len(total) > 1:
                    total = [total[k] + total[k + 1] for k in range(0, len(total), 2)]
                rows[i] = jnp.where(inside, 0.0, rows[i]) - total[0]
        if behind < count:
            across_panel = jnp.concatenate(
                [zeros] * p + block + [zeros] * (count - p - tall), axis=0
            )
            total = dot(jnp.concatenate(rows[behind:], axis=0), across_panel)
            for i in range(behind, count):
                k = SUB * (i - behind)
                rows[i] = jnp.where(inside, 0.0, rows[i]) - total[k : k + SUB, :]
    out = []
    for b in range(count):
        place = lane - (sub + SUB * b)
        unit = jnp.where(place < 0, rows[b], jnp.where(place == 0, 1.0, 0.0))
        out.append(unit * lax.rsqrt(scales[b]))
    return jnp.concatenate(out, axis=0)


def eliminated_slowly(gram):
    row = lax.broadcasted_iota(jnp.int32, (RANK, RANK), 0)
    column = lax.broadcasted_iota(jnp.int32, (RANK, RANK), 1)

    def step(j, a):
        across = jnp.sum(jnp.where(row == j, a, 0.0), axis=0, keepdims=True)
        down = jnp.sum(jnp.where(column == j, a, 0.0), axis=1, keepdims=True)
        pivot = jnp.sum(jnp.where(column == row, jnp.where(row == j, a, 0.0), 0.0))
        across = jnp.where(column == j, 1.0, across) / pivot
        return jnp.where(row > j, jnp.where(column == j, 0.0, a) - down * across, a)

    a = lax.fori_loop(0, RANK, step, gram)
    pivots = jnp.sum(jnp.where(row == column, a, 0.0), axis=1, keepdims=True)
    unit = jnp.where(row > column, a, jnp.where(row == column, 1.0, 0.0))
    return unit * lax.rsqrt(pivots)


def identity():
    row = lax.broadcasted_iota(jnp.int32, (RANK, RANK), 0)
    column = lax.broadcasted_iota(jnp.int32, (RANK, RANK), 1)
    return jnp.where(row == column, 1.0, 0.0)


def half_lower(a):
    row = lax.broadcasted_iota(jnp.int32, (RANK, RANK), 0)
    column = lax.broadcasted_iota(jnp.int32, (RANK, RANK), 1)
    return jnp.where(row > column, a, jnp.where(row == column, 0.5 * a, 0.0))


def series(gram, order):
    error = gram - identity()
    near = jnp.sum(error * error) < NEAR[order]
    first = half_lower(error)
    if order == 1:
        return -first, near
    small = first.astype(jnp.bfloat16)
    square = jnp.dot(small, small, preferred_element_type=jnp.float32)
    outer = lax.dot_general(
        small, small, (((1,), (1,)), ((), ())), preferred_element_type=jnp.float32
    )
    return (square + half_lower(outer)) - first, near


def whole(gram, order):
    return eliminated_slowly(gram) - identity(), None


def two(a):
    high = a.astype(jnp.bfloat16)
    return high, (a - high.astype(jnp.float32)).astype(jnp.bfloat16)


def corrected(change, array, small):
    product = functools.partial(jnp.dot, preferred_element_type=jnp.float32)
    if small:
        return array + product(change.astype(jnp.bfloat16), array.astype(jnp.bfloat16))
    change_high, change_low = two(change)
    high, low = two(array)
    return array + (
        product(change_high, high) + (product(change_high, low) + product(change_low, high))
    )


def unpacked(packed):
    row = lax.broadcasted_iota(jnp.int32, (RANK, RANK), 0)
    column = lax.broadcasted_iota(jnp.int32, (RANK, RANK), 1)
    corner, both = packed[:RANK, :], packed[RANK:DAYS, :]
    flipped = both.T
    diagonal = packed[DAYS : DAYS + 1, :]
    first = jnp.where(row >= column, both, flipped)
    last = jnp.where(row < column, both, jnp.where(row == column, diagonal, flipped))
    return jnp.concatenate(
        [jnp.concatenate([first, corner], axis=1), jnp.concatenate([corner.T, last], axis=1)],
        axis=0,
    )


def outputs(cells, first_factor, second_factor, refs):
    packed_ref, sketch_ref, anomalies_ref, eofs_ref, pcs_ref = refs
    covariance = unpacked(packed_ref[...])
    parts = pieces(covariance)
    sketch = sketch_ref[...]
    seen = dot_right(sketch, parts)
    gram = dot_left(pieces(seen), sketch, ((1,), (1,)))
    inverse = first_factor(gram)
    days = dot(inverse, seen)
    change, first_near = second_factor(dot_nt(days, dot_left(pieces(inverse), sketch)), 1)
    small = second_factor is series
    back = corrected(change, days, small).astype(jnp.bfloat16)
    seen = dot_right(back, parts)
    gram = dot_left(pieces(seen), back, ((1,), (1,)))
    inverse = first_factor(gram)
    rows = dot_left(pieces(inverse), back)
    days = dot(inverse, seen)
    scale = jnp.sqrt(jnp.float32(cells))
    patterns = dot_left(pieces(rows * scale), anomalies_ref[...])
    change, last_near = second_factor(dot_nt(days, rows), 2)
    day_scale = jnp.sqrt(jnp.float32(DAYS) / jnp.float32(cells))
    pcs_ref[...] = corrected(change, days, small) * day_scale
    eofs_ref[...] = corrected(change, patterns, small)
    return first_near, last_near


def algebra(cells, *refs):
    first_near, last_near = outputs(cells, eliminated, series, refs)

    @pl.when(jnp.logical_not(first_near & last_near))
    def _():
        outputs(cells, eliminated_slowly, whole, refs)


def product(anomalies_ref, packed_ref, here, arrived):
    copy = pltpu.make_async_copy(anomalies_ref, here, arrived)
    copy.start()
    copy.wait()
    cells = here[...]
    total = lax.dot_general(
        cells, cells, (((1,), (1,)), ((), ())), preferred_element_type=jnp.float32
    )
    row = lax.broadcasted_iota(jnp.int32, (RANK, RANK), 0)
    column = lax.broadcasted_iota(jnp.int32, (RANK, RANK), 1)
    first, last = total[:RANK, :RANK], total[RANK:, RANK:]
    diagonal = jnp.sum(jnp.where(row == column, last, 0.0), axis=0, keepdims=True)
    packed_ref[:RANK, :] = total[:RANK, RANK:]
    packed_ref[RANK:DAYS, :] = jnp.where(row >= column, first, last)
    spare = lax.broadcasted_iota(jnp.int32, (PACKED - DAYS, RANK), 0)
    packed_ref[DAYS:, :] = jnp.where(spare == 0, diagonal, 0.0)


def all_to_all(array, axes):
    return lax.all_to_all(array, axes, split_axis=0, concat_axis=0, tiled=True)


def sent_to_all(array, axes):
    return all_to_all(jnp.broadcast_to(array, (lax.axis_size(axes), *array.shape)), axes)


def summed(packed):
    shares = packed.reshape(lax.axis_size(LAYER), -1, 1, RANK)
    share = all_to_all(shares, LAYER).sum(axis=0)
    share = sent_to_all(share, "z").sum(axis=0)
    return sent_to_all(share, LAYER).reshape(packed.shape)


def local(anomalies, sketch):
    cells = anomalies.shape[1] * lax.axis_size(CELL_AXES)
    vmem = pl.BlockSpec(memory_space=pltpu.VMEM)
    packed = pl.pallas_call(
        product,
        out_shape=jax.ShapeDtypeStruct((PACKED, RANK), jnp.float32),
        in_specs=[pl.BlockSpec(memory_space=pltpu.HBM)],
        out_specs=vmem,
        scratch_shapes=[pltpu.VMEM(anomalies.shape, anomalies.dtype), pltpu.SemaphoreType.DMA],
        compiler_params=pltpu.CompilerParams(vmem_limit_bytes=PRODUCT_VMEM),
        name="product",
    )(pltpu.with_memory_space_constraint(anomalies, pltpu.HBM))
    return pl.pallas_call(
        functools.partial(algebra, cells),
        out_shape=(
            jax.ShapeDtypeStruct((RANK, anomalies.shape[1]), jnp.float32),
            jax.ShapeDtypeStruct((RANK, DAYS), jnp.float32),
        ),
        in_specs=[vmem, vmem, vmem],
        out_specs=(vmem, vmem),
        compiler_params=pltpu.CompilerParams(vmem_limit_bytes=16 * 2**20),
        name="algebra",
    )(summed(packed), sketch, anomalies)


def solution(mesh):
    split = Mesh(mesh.devices.reshape(4, 4, 8, 2), CELL_AXES)
    in_specs = (P(None, CELL_AXES), P())
    out_specs = (P(None, CELL_AXES), P())
    return jax.shard_map(local, mesh=split, in_specs=in_specs, out_specs=out_specs, check_vma=False)
```

```python
import functools

import jax
import jax.numpy as jnp
from jax import lax
from jax.experimental import pallas as pl
from jax.experimental.pallas import tpu as pltpu
from jax.sharding import Mesh
from jax.sharding import PartitionSpec as P

LAYER = ("y", "x")
CELL_AXES = ("y", "x", "z", "core")
RANK = 128
DAYS = 256
PRODUCT_VMEM = 8 * 2**20
PACKED = 288
SUB = 8
PANEL = 16
NEAR = {1: 1e-7, 2: 2e-5}
HIGHEST = lax.Precision.HIGHEST


def dot(a, b, dims=((1,), (0,))):
    return lax.dot_general(
        a, b, (dims, ((), ())), precision=HIGHEST, preferred_element_type=jnp.float32
    )


def dot_nt(a, b):
    return dot(a, b, ((1,), (1,)))


def pieces(a):
    high = a.astype(jnp.bfloat16)
    rest = a - high.astype(jnp.float32)
    middle = rest.astype(jnp.bfloat16)
    low = (rest - middle.astype(jnp.float32)).astype(jnp.bfloat16)
    return high, middle, low


def dot_right(a, split, dims=((1,), (0,))):
    high, middle, low = (
        lax.dot_general(a, b, (dims, ((), ())), preferred_element_type=jnp.float32) for b in split
    )
    return high + (middle + low)


def dot_left(split, b, dims=((1,), (0,))):
    high, middle, low = (
        lax.dot_general(a, b, (dims, ((), ())), preferred_element_type=jnp.float32) for a in split
    )
    return high + (middle + low)


def spread(a):
    return jnp.broadcast_to(a, (SUB, RANK))


def eliminated(gram):
    lane = lax.broadcasted_iota(jnp.int32, (SUB, RANK), 1)
    sub = lax.broadcasted_iota(jnp.int32, (SUB, RANK), 0)
    at = [sub == s for s in range(SUB)]
    count, tall = RANK // SUB, PANEL // SUB
    rows = [gram[SUB * b : SUB * (b + 1), :] for b in range(count)]
    zeros = jnp.zeros((SUB, RANK), jnp.float32)
    scales = []
    for p in range(0, count, tall):
        j = SUB * p
        block = rows[p : p + tall]
        kept, scale = list(block), [jnp.ones((SUB, RANK), jnp.float32)] * tall
        columns = [[spread(a[:, j + u : j + u + 1]) for a in block] for u in range(PANEL)]
        pivot = spread(columns[0][0][0:1, :])
        for t in range(PANEL):
            own, s = divmod(t, SUB)
            inverse = 1.0 / pivot
            scale[own] = jnp.where(at[s], pivot, scale[own])
            across = {v: spread(columns[v][own][s : s + 1, :]) for v in range(t + 1, PANEL)}
            if t + 1 < PANEL:
                b, r = divmod(t + 1, SUB)
                corner = spread(columns[t + 1][b][r : r + 1, :])
                pivot = corner - (across[t + 1] * across[t + 1]) * inverse
            row = spread(block[own][s : s + 1, :])
            kept[own] = jnp.where(at[s], row, kept[own])
            here = lane == j + t
            row = jnp.where(here, 1.0, row) * inverse
            for k in range(tall):
                changed = jnp.where(here, 0.0, block[k]) - columns[t][k] * row
                block[k] = jnp.where(at[s], row, changed) if k == own else changed
            for v in range(t + 1, PANEL):
                ratio = across[v] * inverse
                for k in range(tall):
                    changed = columns[v][k] - columns[t][k] * ratio
                    columns[v][k] = jnp.where(at[s], ratio, changed) if k == own else changed
        rows[p : p + tall] = kept
        scales += scale
        inside = (lane >= j) & (lane < j + PANEL)
        behind = p + 2 * tall
        if p + tall < count:
            solved = [spread(block[u // SUB][u % SUB : u % SUB + 1, :]) for u in range(PANEL)]
            terms = {
                i: [spread(rows[i][:, j + u : j + u + 1]) * solved[u] for u in range(PANEL)]
                for i in range(p + tall, behind)
            }
            for i, total in terms.items():
                while len(total) > 1:
                    total = [total[k] + total[k + 1] for k in range(0, len(total), 2)]
                rows[i] = jnp.where(inside, 0.0, rows[i]) - total[0]
        if behind < count:
            across_panel = jnp.concatenate(
                [zeros] * p + block + [zeros] * (count - p - tall), axis=0
            )
            total = dot(jnp.concatenate(rows[behind:], axis=0), across_panel)
            for i in range(behind, count):
                k = SUB * (i - behind)
                rows[i] = jnp.where(inside, 0.0, rows[i]) - total[k : k + SUB, :]
    out = []
    for b in range(count):
        place = lane - (sub + SUB * b)
        unit = jnp.where(place < 0, rows[b], jnp.where(place == 0, 1.0, 0.0))
        out.append(unit * lax.rsqrt(scales[b]))
    return jnp.concatenate(out, axis=0)


def eliminated_slowly(gram):
    row = lax.broadcasted_iota(jnp.int32, (RANK, RANK), 0)
    column = lax.broadcasted_iota(jnp.int32, (RANK, RANK), 1)

    def step(j, a):
        across = jnp.sum(jnp.where(row == j, a, 0.0), axis=0, keepdims=True)
        down = jnp.sum(jnp.where(column == j, a, 0.0), axis=1, keepdims=True)
        pivot = jnp.sum(jnp.where(column == row, jnp.where(row == j, a, 0.0), 0.0))
        across = jnp.where(column == j, 1.0, across) / pivot
        return jnp.where(row > j, jnp.where(column == j, 0.0, a) - down * across, a)

    a = lax.fori_loop(0, RANK, step, gram)
    pivots = jnp.sum(jnp.where(row == column, a, 0.0), axis=1, keepdims=True)
    unit = jnp.where(row > column, a, jnp.where(row == column, 1.0, 0.0))
    return unit * lax.rsqrt(pivots)


def identity():
    row = lax.broadcasted_iota(jnp.int32, (RANK, RANK), 0)
    column = lax.broadcasted_iota(jnp.int32, (RANK, RANK), 1)
    return jnp.where(row == column, 1.0, 0.0)


def half_lower(a):
    row = lax.broadcasted_iota(jnp.int32, (RANK, RANK), 0)
    column = lax.broadcasted_iota(jnp.int32, (RANK, RANK), 1)
    return jnp.where(row > column, a, jnp.where(row == column, 0.5 * a, 0.0))


def series(gram, order):
    error = gram - identity()
    near = jnp.sum(error * error) < NEAR[order]
    first = half_lower(error)
    if order == 1:
        return -first, near
    small = first.astype(jnp.bfloat16)
    square = jnp.dot(small, small, preferred_element_type=jnp.float32)
    outer = lax.dot_general(
        small, small, (((1,), (1,)), ((), ())), preferred_element_type=jnp.float32
    )
    return (square + half_lower(outer)) - first, near


def whole(gram, order):
    return eliminated_slowly(gram) - identity(), None


def two(a):
    high = a.astype(jnp.bfloat16)
    return high, (a - high.astype(jnp.float32)).astype(jnp.bfloat16)


def corrected(change, array, small):
    product = functools.partial(jnp.dot, preferred_element_type=jnp.float32)
    if small:
        return array + product(change.astype(jnp.bfloat16), array.astype(jnp.bfloat16))
    change_high, change_low = two(change)
    high, low = two(array)
    return array + (
        product(change_high, high) + (product(change_high, low) + product(change_low, high))
    )


def unpacked(packed):
    row = lax.broadcasted_iota(jnp.int32, (RANK, RANK), 0)
    column = lax.broadcasted_iota(jnp.int32, (RANK, RANK), 1)
    corner, both = packed[:RANK, :], packed[RANK:DAYS, :]
    flipped = both.T
    diagonal = packed[DAYS : DAYS + 1, :]
    first = jnp.where(row >= column, both, flipped)
    last = jnp.where(row < column, both, jnp.where(row == column, diagonal, flipped))
    return jnp.concatenate(
        [jnp.concatenate([first, corner], axis=1), jnp.concatenate([corner.T, last], axis=1)],
        axis=0,
    )


def outputs(cells, first_factor, second_factor, refs):
    packed_ref, sketch_ref, anomalies_ref, eofs_ref, pcs_ref = refs
    covariance = unpacked(packed_ref[...])
    parts = pieces(covariance)
    sketch = sketch_ref[...]
    seen = dot_right(sketch, parts)
    gram = dot_left(pieces(seen), sketch, ((1,), (1,)))
    inverse = first_factor(gram)
    days = dot(inverse, seen)
    change, first_near = second_factor(dot_nt(days, dot_left(pieces(inverse), sketch)), 1)
    small = second_factor is series
    back = corrected(change, days, small).astype(jnp.bfloat16)
    seen = dot_right(back, parts)
    gram = dot_left(pieces(seen), back, ((1,), (1,)))
    inverse = first_factor(gram)
    rows = dot_left(pieces(inverse), back)
    days = dot(inverse, seen)
    scale = jnp.sqrt(jnp.float32(cells))
    patterns = dot_left(pieces(rows * scale), anomalies_ref[...])
    change, last_near = second_factor(dot_nt(days, rows), 2)
    day_scale = jnp.sqrt(jnp.float32(DAYS) / jnp.float32(cells))
    pcs_ref[...] = corrected(change, days, small) * day_scale
    eofs_ref[...] = corrected(change, patterns, small)
    return first_near, last_near


def algebra(cells, *refs):
    first_near, last_near = outputs(cells, eliminated, series, refs)

    @pl.when(jnp.logical_not(first_near & last_near))
    def _():
        outputs(cells, eliminated_slowly, whole, refs)


def product(anomalies_ref, packed_ref, here, arrived):
    copy = pltpu.make_async_copy(anomalies_ref, here, arrived)
    copy.start()
    copy.wait()
    cells = here[...]
    total = lax.dot_general(
        cells, cells, (((1,), (1,)), ((), ())), preferred_element_type=jnp.float32
    )
    row = lax.broadcasted_iota(jnp.int32, (RANK, RANK), 0)
    column = lax.broadcasted_iota(jnp.int32, (RANK, RANK), 1)
    first, last = total[:RANK, :RANK], total[RANK:, RANK:]
    diagonal = jnp.sum(jnp.where(row == column, last, 0.0), axis=0, keepdims=True)
    packed_ref[:RANK, :] = total[:RANK, RANK:]
    packed_ref[RANK:DAYS, :] = jnp.where(row >= column, first, last)
    spare = lax.broadcasted_iota(jnp.int32, (PACKED - DAYS, RANK), 0)
    packed_ref[DAYS:, :] = jnp.where(spare == 0, diagonal, 0.0)


def all_to_all(array, axes):
    return lax.all_to_all(array, axes, split_axis=0, concat_axis=0, tiled=True)


def sent_to_all(array, axes):
    return all_to_all(jnp.broadcast_to(array, (lax.axis_size(axes), *array.shape)), axes)


def summed(packed):
    shares = packed.reshape(lax.axis_size(LAYER), -1, 2, RANK)
    share = all_to_all(shares, LAYER).sum(axis=0)
    share = share + lax.ppermute(share, "core", [(0, 1), (1, 0)])
    share = sent_to_all(share, "z").sum(axis=0)
    return sent_to_all(share, LAYER).reshape(packed.shape)


def local(anomalies, sketch):
    cells = anomalies.shape[1] * lax.axis_size(CELL_AXES)
    vmem = pl.BlockSpec(memory_space=pltpu.VMEM)
    packed = pl.pallas_call(
        product,
        out_shape=jax.ShapeDtypeStruct((PACKED, RANK), jnp.float32),
        in_specs=[pl.BlockSpec(memory_space=pltpu.HBM)],
        out_specs=vmem,
        scratch_shapes=[pltpu.VMEM(anomalies.shape, anomalies.dtype), pltpu.SemaphoreType.DMA],
        compiler_params=pltpu.CompilerParams(vmem_limit_bytes=PRODUCT_VMEM),
        name="product",
    )(pltpu.with_memory_space_constraint(anomalies, pltpu.HBM))
    return pl.pallas_call(
        functools.partial(algebra, cells),
        out_shape=(
            jax.ShapeDtypeStruct((RANK, anomalies.shape[1]), jnp.float32),
            jax.ShapeDtypeStruct((RANK, DAYS), jnp.float32),
        ),
        in_specs=[vmem, vmem, vmem],
        out_specs=(vmem, vmem),
        compiler_params=pltpu.CompilerParams(vmem_limit_bytes=16 * 2**20),
        name="algebra",
    )(summed(packed), sketch, anomalies)


def solution(mesh):
    split = Mesh(mesh.devices.reshape(4, 4, 8, 2), CELL_AXES)
    in_specs = (P(None, CELL_AXES), P())
    out_specs = (P(None, CELL_AXES), P())
    return jax.shard_map(local, mesh=split, in_specs=in_specs, out_specs=out_specs, check_vma=False)
```

```python
import functools

import jax
import jax.numpy as jnp
from jax import lax
from jax.experimental import pallas as pl
from jax.experimental.pallas import tpu as pltpu
from jax.sharding import Mesh
from jax.sharding import PartitionSpec as P

LAYER = ("y", "x")
CELL_AXES = ("y", "x", "z", "core")
RANK = 128
DAYS = 256
PRODUCT_VMEM = 8 * 2**20
PACKED = 288
SUB = 8
PANEL = 16
NEAR = {1: 1e-7, 2: 2e-5}
HIGHEST = lax.Precision.HIGHEST


def dot(a, b, dims=((1,), (0,))):
    return lax.dot_general(
        a, b, (dims, ((), ())), precision=HIGHEST, preferred_element_type=jnp.float32
    )


def dot_nt(a, b):
    return dot(a, b, ((1,), (1,)))


def pieces(a):
    high = a.astype(jnp.bfloat16)
    rest = a - high.astype(jnp.float32)
    middle = rest.astype(jnp.bfloat16)
    low = (rest - middle.astype(jnp.float32)).astype(jnp.bfloat16)
    return high, middle, low


def dot_right(a, split, dims=((1,), (0,))):
    high, middle, low = (
        lax.dot_general(a, b, (dims, ((), ())), preferred_element_type=jnp.float32) for b in split
    )
    return high + (middle + low)


def dot_left(split, b, dims=((1,), (0,))):
    high, middle, low = (
        lax.dot_general(a, b, (dims, ((), ())), preferred_element_type=jnp.float32) for a in split
    )
    return high + (middle + low)


def spread(a):
    return jnp.broadcast_to(a, (SUB, RANK))


def eliminated(gram):
    lane = lax.broadcasted_iota(jnp.int32, (SUB, RANK), 1)
    sub = lax.broadcasted_iota(jnp.int32, (SUB, RANK), 0)
    at = [sub == s for s in range(SUB)]
    count, tall = RANK // SUB, PANEL // SUB
    rows = [gram[SUB * b : SUB * (b + 1), :] for b in range(count)]
    zeros = jnp.zeros((SUB, RANK), jnp.float32)
    scales = []
    for p in range(0, count, tall):
        j = SUB * p
        block = rows[p : p + tall]
        kept, scale = list(block), [jnp.ones((SUB, RANK), jnp.float32)] * tall
        columns = [[spread(a[:, j + u : j + u + 1]) for a in block] for u in range(PANEL)]
        pivot = spread(columns[0][0][0:1, :])
        for t in range(PANEL):
            own, s = divmod(t, SUB)
            inverse = 1.0 / pivot
            scale[own] = jnp.where(at[s], pivot, scale[own])
            across = {v: spread(columns[v][own][s : s + 1, :]) for v in range(t + 1, PANEL)}
            if t + 1 < PANEL:
                b, r = divmod(t + 1, SUB)
                corner = spread(columns[t + 1][b][r : r + 1, :])
                pivot = corner - (across[t + 1] * across[t + 1]) * inverse
            row = spread(block[own][s : s + 1, :])
            kept[own] = jnp.where(at[s], row, kept[own])
            here = lane == j + t
            row = jnp.where(here, 1.0, row) * inverse
            for k in range(own, tall):
                changed = jnp.where(here, 0.0, block[k]) - columns[t][k] * row
                block[k] = jnp.where(at[s], row, changed) if k == own else changed
            for v in range(t + 1, PANEL):
                ratio = across[v] * inverse
                for k in range(own, tall):
                    changed = columns[v][k] - columns[t][k] * ratio
                    columns[v][k] = jnp.where(at[s], ratio, changed) if k == own else changed
        terms = [columns[SUB + t][0] * spread(block[1][t : t + 1, :]) for t in range(SUB)]
        while len(terms) > 1:
            terms = [terms[k] + terms[k + 1] for k in range(0, len(terms), 2)]
        upper = (lane >= j + SUB) & (lane < j + PANEL)
        block[0] = jnp.where(upper, 0.0, block[0]) - terms[0]
        rows[p : p + tall] = kept
        scales += scale
        inside = (lane >= j) & (lane < j + PANEL)
        behind = p + 2 * tall
        if p + tall < count:
            solved = [spread(block[u // SUB][u % SUB : u % SUB + 1, :]) for u in range(PANEL)]
            terms = {
                i: [spread(rows[i][:, j + u : j + u + 1]) * solved[u] for u in range(PANEL)]
                for i in range(p + tall, behind)
            }
            for i, total in terms.items():
                while len(total) > 1:
                    total = [total[k] + total[k + 1] for k in range(0, len(total), 2)]
                rows[i] = jnp.where(inside, 0.0, rows[i]) - total[0]
        if behind < count:
            across_panel = jnp.concatenate(
                [zeros] * p + block + [zeros] * (count - p - tall), axis=0
            )
            total = dot(jnp.concatenate(rows[behind:], axis=0), across_panel)
            for i in range(behind, count):
                k = SUB * (i - behind)
                rows[i] = jnp.where(inside, 0.0, rows[i]) - total[k : k + SUB, :]
    out = []
    for b in range(count):
        place = lane - (sub + SUB * b)
        unit = jnp.where(place < 0, rows[b], jnp.where(place == 0, 1.0, 0.0))
        out.append(unit * lax.rsqrt(scales[b]))
    return jnp.concatenate(out, axis=0)


def eliminated_slowly(gram):
    row = lax.broadcasted_iota(jnp.int32, (RANK, RANK), 0)
    column = lax.broadcasted_iota(jnp.int32, (RANK, RANK), 1)

    def step(j, a):
        across = jnp.sum(jnp.where(row == j, a, 0.0), axis=0, keepdims=True)
        down = jnp.sum(jnp.where(column == j, a, 0.0), axis=1, keepdims=True)
        pivot = jnp.sum(jnp.where(column == row, jnp.where(row == j, a, 0.0), 0.0))
        across = jnp.where(column == j, 1.0, across) / pivot
        return jnp.where(row > j, jnp.where(column == j, 0.0, a) - down * across, a)

    a = lax.fori_loop(0, RANK, step, gram)
    pivots = jnp.sum(jnp.where(row == column, a, 0.0), axis=1, keepdims=True)
    unit = jnp.where(row > column, a, jnp.where(row == column, 1.0, 0.0))
    return unit * lax.rsqrt(pivots)


def identity():
    row = lax.broadcasted_iota(jnp.int32, (RANK, RANK), 0)
    column = lax.broadcasted_iota(jnp.int32, (RANK, RANK), 1)
    return jnp.where(row == column, 1.0, 0.0)


def half_lower(a):
    row = lax.broadcasted_iota(jnp.int32, (RANK, RANK), 0)
    column = lax.broadcasted_iota(jnp.int32, (RANK, RANK), 1)
    return jnp.where(row > column, a, jnp.where(row == column, 0.5 * a, 0.0))


def series(gram, order):
    error = gram - identity()
    near = jnp.sum(error * error) < NEAR[order]
    first = half_lower(error)
    if order == 1:
        return -first, near
    small = first.astype(jnp.bfloat16)
    square = jnp.dot(small, small, preferred_element_type=jnp.float32)
    outer = lax.dot_general(
        small, small, (((1,), (1,)), ((), ())), preferred_element_type=jnp.float32
    )
    return (square + half_lower(outer)) - first, near


def whole(gram, order):
    return eliminated_slowly(gram) - identity(), None


def two(a):
    high = a.astype(jnp.bfloat16)
    return high, (a - high.astype(jnp.float32)).astype(jnp.bfloat16)


def corrected(change, array, small):
    product = functools.partial(jnp.dot, preferred_element_type=jnp.float32)
    if small:
        return array + product(change.astype(jnp.bfloat16), array.astype(jnp.bfloat16))
    change_high, change_low = two(change)
    high, low = two(array)
    return array + (
        product(change_high, high) + (product(change_high, low) + product(change_low, high))
    )


def unpacked(packed):
    row = lax.broadcasted_iota(jnp.int32, (RANK, RANK), 0)
    column = lax.broadcasted_iota(jnp.int32, (RANK, RANK), 1)
    corner, both = packed[:RANK, :], packed[RANK:DAYS, :]
    flipped = both.T
    diagonal = packed[DAYS : DAYS + 1, :]
    first = jnp.where(row >= column, both, flipped)
    last = jnp.where(row < column, both, jnp.where(row == column, diagonal, flipped))
    return jnp.concatenate(
        [jnp.concatenate([first, corner], axis=1), jnp.concatenate([corner.T, last], axis=1)],
        axis=0,
    )


def outputs(cells, first_factor, second_factor, refs):
    packed_ref, sketch_ref, anomalies_ref, eofs_ref, pcs_ref = refs
    covariance = unpacked(packed_ref[...])
    parts = pieces(covariance)
    sketch = sketch_ref[...]
    seen = dot_right(sketch, parts)
    gram = dot_left(pieces(seen), sketch, ((1,), (1,)))
    inverse = first_factor(gram)
    days = dot(inverse, seen)
    change, first_near = second_factor(dot_nt(days, dot_left(pieces(inverse), sketch)), 1)
    small = second_factor is series
    back = corrected(change, days, small).astype(jnp.bfloat16)
    seen = dot_right(back, parts)
    gram = dot_left(pieces(seen), back, ((1,), (1,)))
    inverse = first_factor(gram)
    rows = dot_left(pieces(inverse), back)
    days = dot(inverse, seen)
    scale = jnp.sqrt(jnp.float32(cells))
    patterns = dot_left(pieces(rows * scale), anomalies_ref[...])
    change, last_near = second_factor(dot_nt(days, rows), 2)
    day_scale = jnp.sqrt(jnp.float32(DAYS) / jnp.float32(cells))
    pcs_ref[...] = corrected(change, days, small) * day_scale
    eofs_ref[...] = corrected(change, patterns, small)
    return first_near, last_near


def algebra(cells, *refs):
    first_near, last_near = outputs(cells, eliminated, series, refs)

    @pl.when(jnp.logical_not(first_near & last_near))
    def _():
        outputs(cells, eliminated_slowly, whole, refs)


def product(anomalies_ref, packed_ref, here, arrived):
    copy = pltpu.make_async_copy(anomalies_ref, here, arrived)
    copy.start()
    copy.wait()
    cells = here[...]
    total = lax.dot_general(
        cells, cells, (((1,), (1,)), ((), ())), preferred_element_type=jnp.float32
    )
    row = lax.broadcasted_iota(jnp.int32, (RANK, RANK), 0)
    column = lax.broadcasted_iota(jnp.int32, (RANK, RANK), 1)
    first, last = total[:RANK, :RANK], total[RANK:, RANK:]
    diagonal = jnp.sum(jnp.where(row == column, last, 0.0), axis=0, keepdims=True)
    packed_ref[:RANK, :] = total[:RANK, RANK:]
    packed_ref[RANK:DAYS, :] = jnp.where(row >= column, first, last)
    spare = lax.broadcasted_iota(jnp.int32, (PACKED - DAYS, RANK), 0)
    packed_ref[DAYS:, :] = jnp.where(spare == 0, diagonal, 0.0)


def all_to_all(array, axes):
    return lax.all_to_all(array, axes, split_axis=0, concat_axis=0, tiled=True)


def sent_to_all(array, axes):
    return all_to_all(jnp.broadcast_to(array, (lax.axis_size(axes), *array.shape)), axes)


def summed(packed):
    shares = packed.reshape(lax.axis_size(LAYER), -1, 2, RANK)
    share = all_to_all(shares, LAYER).sum(axis=0)
    share = share + lax.ppermute(share, "core", [(0, 1), (1, 0)])
    share = sent_to_all(share, "z").sum(axis=0)
    return sent_to_all(share, LAYER).reshape(packed.shape)


def local(anomalies, sketch):
    cells = anomalies.shape[1] * lax.axis_size(CELL_AXES)
    vmem = pl.BlockSpec(memory_space=pltpu.VMEM)
    packed = pl.pallas_call(
        product,
        out_shape=jax.ShapeDtypeStruct((PACKED, RANK), jnp.float32),
        in_specs=[pl.BlockSpec(memory_space=pltpu.HBM)],
        out_specs=vmem,
        scratch_shapes=[pltpu.VMEM(anomalies.shape, anomalies.dtype), pltpu.SemaphoreType.DMA],
        compiler_params=pltpu.CompilerParams(vmem_limit_bytes=PRODUCT_VMEM),
        name="product",
    )(pltpu.with_memory_space_constraint(anomalies, pltpu.HBM))
    return pl.pallas_call(
        functools.partial(algebra, cells),
        out_shape=(
            jax.ShapeDtypeStruct((RANK, anomalies.shape[1]), jnp.float32),
            jax.ShapeDtypeStruct((RANK, DAYS), jnp.float32),
        ),
        in_specs=[vmem, vmem, vmem],
        out_specs=(vmem, vmem),
        compiler_params=pltpu.CompilerParams(vmem_limit_bytes=16 * 2**20),
        name="algebra",
    )(summed(packed), sketch, anomalies)


def solution(mesh):
    split = Mesh(mesh.devices.reshape(4, 4, 8, 2), CELL_AXES)
    in_specs = (P(None, CELL_AXES), P())
    out_specs = (P(None, CELL_AXES), P())
    return jax.shard_map(local, mesh=split, in_specs=in_specs, out_specs=out_specs, check_vma=False)
```
